256 devices in a mesh: space: 32 (over y, x, core), tm: 8 (over z).
Axes of the slice: x: 4, y: 4, z: 8, core: 2. Of those that a mesh axis runs over, the one named last changes fastest.
Arguments:
- forcing: float32 [16, 768, 20, 128], P('tm', 'space'), may hold values from -6 to 6
- observed: float32 [16, 768, 20, 128], P('tm', 'space'), may hold values from -6 to 6
- jacobian: bfloat16 [16, 768, 7, 128, 128], P('tm', 'space'), may hold values from -0.078125 to 0.078125
- block_index: int32 [768, 7], P('space'), may hold values from 0 to 27, as said below
- send_list: int32 [128, 1], P('space'), may hold values from 0 to 23
- damping: float32 [768, 128], P('space'), may hold values from 0.5 to 0.9
- error_weight: float32 [768, 128], P('space'), may hold values from 0.5 to 2
- forcing_weight: float32 [128], replicated, may hold values from 0.5 to 2
Outputs:
- trajectory: float32 [16, 768, 20, 128], P('tm', 'space')
- gradient: float32 [16, 768, 20, 128], P('tm', 'space')
The draws below stay inside these ranges and needn't reach their ends.
Inputs may be any that keep to these rules, and one draw needn't show every extreme that they name: `block_index`: block 0 of every column reads the column itself; each received column is read by exactly one block of its partition.
All inputs are finite; a program needn't handle non-finite values.
Results may differ from the reference program's by a relative error of at most 0.0045.
Values may be sent and summed in bfloat16 or wider, within the bound.
No kernel may reach another device: no remote copies, remote signals or barrier semaphores. Data moves between devices by JAX's collectives and lax.ppermute only.
A program may use at most 64 MiB of HBM per device.

```python
import math
import jax
import jax.numpy as jnp
from jax import lax

LEV = 128
NEIGH = 7
HOPS = 4
COLS_DEV = 24
MEMBERS = 20
BORDER = 1
COLS = 768
STEPS = 16
N_SPACE = 32


def draw_block_index(key, part):
    local = jax.random.randint(key, (COLS, NEIGH), 0, COLS_DEV, dtype=jnp.int32)
    column = (jnp.arange(COLS, dtype=jnp.int32) % COLS_DEV)[:, None]
    blocks = jnp.arange(NEIGH, dtype=jnp.int32)[None, :]
    slot = column + COLS_DEV * (NEIGH - 1 - blocks)
    received = HOPS * BORDER
    chosen = jnp.where(blocks == 0, column, local)
    return jnp.where(slot < received, COLS_DEV + slot, chosen).astype(jnp.int32)


def set_ends(values, key, least, largest):
    spot = [jax.random.randint(jax.random.fold_in(key, axis), (), 0, length) for axis, length in enumerate(values.shape)]
    widest = values.shape.index(max(values.shape))
    next_to = spot[:widest] + [(spot[widest] + 1) % values.shape[widest]] + spot[widest + 1:]
    return values.at[tuple(spot)].set(least).at[tuple(next_to)].set(largest)


def levels(own_key, dims, shards, low, high):
    level = 1.0
    for dim, parts in shards:
        heights = jax.random.uniform(jax.random.fold_in(jax.random.fold_in(own_key, 6), dim), (parts,), jnp.float32, low / len(shards), high / len(shards))
        level = level * jnp.repeat(jnp.exp(heights), dims[dim] // parts).reshape((-1,) + (1,) * (len(dims) - 1 - dim))
    return level


def scatter_about(own_key, dims, width, bound, shards=(), held_as=jnp.bfloat16):
    values = width * jax.random.normal(own_key, dims, jnp.float32)
    if shards:
        values = values * levels(own_key, dims, shards, -0.22, 0.18)
    return jnp.clip(values, -bound, bound).astype(held_as)


def setup_inputs(seed: int = 0) -> dict:
    arg_keys = jax.random.split(jax.random.key(seed), 9)
    forcing = scatter_about(arg_keys[0], (STEPS, COLS, MEMBERS, LEV), 1.0, 6.0, ((0, 8), (1, 32)), jnp.float32)
    observed = scatter_about(arg_keys[1], (STEPS, COLS, MEMBERS, LEV), 1.0, 6.0, ((0, 8), (1, 32)), jnp.float32)
    jacobian = scatter_about(arg_keys[2], (STEPS, COLS, NEIGH, LEV, LEV), (6 * LEV * NEIGH) ** -0.5, 0.078125, ((0, 8), (1, 32)))
    block_index = draw_block_index(jax.random.fold_in(arg_keys[8], 71), 0)
    send_list = set_ends(jax.random.randint(arg_keys[4], (N_SPACE * HOPS, BORDER), 0, COLS_DEV), jax.random.fold_in(arg_keys[4], 1), 0, COLS_DEV - 1).astype(jnp.int32)
    damping = jnp.clip(0.5 + 0.39999998 * jax.random.uniform(arg_keys[5], (COLS, LEV), jnp.float32) ** levels(arg_keys[5], (COLS, LEV), ((0, 32),), -0.2, 0.2), 0.5, 0.9)
    error_weight = jnp.clip(jnp.exp(math.log(2.0) - 1.3862944 * jax.random.uniform(arg_keys[6], (COLS, LEV), jnp.float32) ** levels(arg_keys[6], (COLS, LEV), ((0, 32),), -0.2, 0.2)), 0.5, 2.0)
    forcing_weight = jnp.clip(jnp.exp(jax.random.uniform(arg_keys[7], (LEV,), jnp.float32, math.log(0.5), math.log(2.0))), 0.5, 2.0)
    return {"forcing": forcing, "observed": observed, "jacobian": jacobian, "block_index": block_index, "send_list": send_list, "damping": damping, "error_weight": error_weight, "forcing_weight": forcing_weight}


def sources(block_index, send_list):
    offsets = jnp.array([1, -1, 2, -2], dtype=jnp.int32)
    part = (jnp.arange(COLS, dtype=jnp.int32) // COLS_DEV)[:, None]
    local = block_index < COLS_DEV
    remote = jnp.maximum(block_index - COLS_DEV, 0)
    hop_id = remote // BORDER
    within = remote % BORDER
    anchor = jnp.mod(part - offsets[hop_id], N_SPACE).astype(jnp.int32)
    remote_col = send_list[anchor * HOPS + hop_id, within]
    return jnp.where(local, part * COLS_DEV + block_index, anchor * COLS_DEV + remote_col).astype(jnp.int32)


def reference(forcing, observed, jacobian, block_index, send_list, damping, error_weight, forcing_weight):
    source = sources(block_index, send_list)

    def forward(current, inputs):
        blocks, push = inputs
        rounded = current.astype(jnp.bfloat16).astype(jnp.float32)
        picked = rounded[source]
        mixed = jnp.einsum("ckmj,ckij->cmi", picked, blocks.astype(jnp.float32))
        result = damping[:, None, :] * current + mixed + push
        return result, result

    start = jnp.zeros(forcing.shape[1:], jnp.float32)
    last_state, trajectory = lax.scan(forward, start, (jacobian, forcing))
    misfit = error_weight[None, :, None, :] * (trajectory - observed)

    def backward(carried, inputs):
        blocks, miss = inputs
        adjoint = miss + carried
        rounded = adjoint.astype(jnp.bfloat16).astype(jnp.float32)
        spread = jnp.einsum("cmi,ckij->ckmj", rounded, blocks.astype(jnp.float32))
        summed = jax.ops.segment_sum(spread.reshape((-1,) + adjoint.shape[1:]), source.reshape(-1), num_segments=COLS)
        return damping[:, None, :] * adjoint + summed, adjoint

    last_term, adjoints = lax.scan(backward, start, (jacobian, misfit), reverse=True)
    gradient = forcing_weight * forcing + adjoints
    return trajectory, gradient
```

```python
import functools

import jax
import jax.numpy as jnp
from jax import lax
from jax.experimental import pallas as pl
from jax.experimental.pallas import tpu as pltpu
from jax.sharding import PartitionSpec as P

OFFSETS = (1, -1, 2, -2)
HOPS = len(OFFSETS)
UNROLL = 6
HALF = jnp.bfloat16
F32 = jnp.float32

VMEM = pl.BlockSpec(memory_space=pltpu.VMEM)
SMEM = pl.BlockSpec(memory_space=pltpu.SMEM)


class Table:
    def __init__(self, columns, blocks):
        self.blocks = blocks
        self.listed = columns * blocks
        self.reader = self.listed + HOPS
        self.block = self.reader + HOPS
        self.first = self.block + HOPS
        self.turn = self.first + HOPS


def dot_t(x, w):
    return lax.dot_general(x, w, (((1,), (1,)), ((), ())), preferred_element_type=F32)


def dot_n(x, w):
    return lax.dot_general(x, w, (((1,), (0,)), ((), ())), preferred_element_type=F32)


def row_of(jac, step, c, blocks):
    return jnp.concatenate([jac[step, c, k] for k in range(blocks)], axis=1)


def gathered(source, table, c, blocks):
    return jnp.concatenate([source[table[c * blocks + k]] for k in range(blocks)], axis=1)


def unpack(packed, members, write):
    def body(i, carry):
        both = packed[pl.ds(pl.multiple_of(i * 2 * members, 8), 2 * members), :]
        write(2 * i, both[:members])
        write(2 * i + 1, both[members:])
        return carry

    lax.fori_loop(0, packed.shape[0] // members // 2, body, 0)


def pack(packed, members, read):
    def body(i, carry):
        both = jnp.concatenate([read(2 * i), read(2 * i + 1)], axis=0)
        packed[pl.ds(pl.multiple_of(i * 2 * members, 8), 2 * members), :] = both
        return carry

    lax.fori_loop(0, packed.shape[0] // members // 2, body, 0)


def over_columns(columns, visit):
    def body(i, carry):
        for j in range(UNROLL):
            visit(i * UNROLL + j)
        return carry

    lax.fori_loop(0, columns // UNROLL, body, 0)


def enter_kernel(turn, at, own, borders, table, damp, push, jac, state, half, *sent):
    columns, members, _ = state.shape

    @pl.when(table[at.turn] == turn)
    def _():
        def write(c, value):
            state[c] = value
            half[c] = value.astype(HALF)

        unpack(own, members, write)
        for h in range(HOPS):
            half[columns + h] = borders[HOPS - 1 - h]
        for h in range(HOPS):
            c = table[at.listed + h]
            mixed = dot_t(gathered(half, table, c, at.blocks), row_of(jac, 0, c, at.blocks))
            sent[h][...] = (damp[pl.ds(c, 1), :] * state[c] + mixed + push[0, c]).astype(HALF)


def advance_kernel(turn, at, state, half, table, damp, push, jac, _, states, half2):
    columns = state.shape[0]

    @pl.when(table[at.turn] == turn)
    def _():
        def first(c):
            mixed = dot_t(gathered(half, table, c, at.blocks), row_of(jac, 0, c, at.blocks))
            value = damp[pl.ds(c, 1), :] * state[c] + mixed + push[0, c]
            states[0, c] = value
            half2[c] = value.astype(HALF)

        over_columns(columns, first)
        half2[columns:] = jnp.zeros((HOPS,) + half2.shape[1:], HALF)

        def second(c):
            mixed = dot_t(gathered(half2, table, c, at.blocks), row_of(jac, 1, c, at.blocks))
            states[1, c] = damp[pl.ds(c, 1), :] * states[0, c] + mixed + push[1, c]

        over_columns(columns, second)


def leave_kernel(turn, at, r3, r2, r1, r0, table, jac, _, states, own, *sent):
    members = states.shape[2]

    @pl.when(table[at.turn] == turn)
    def _():
        for h, border in enumerate((r0, r1, r2, r3)):
            c = table[at.reader + h]
            states[1, c] = states[1, c] + dot_t(border[...], jac[1, c, table[at.block + h]])
        pack(own, members, lambda c: states[1, c])
        for h in range(HOPS):
            sent[h][...] = states[1, table[at.listed + h]].astype(HALF)


def enter_back_kernel(
    turn, at, own, terms, table, states, observed, weight, jac, _, values, half, *sent
):
    members = states.shape[2]

    @pl.when(table[at.turn] == turn)
    def _():
        def write(c, value):
            values[1, c] = value + weight[pl.ds(c, 1), :] * (states[1, c] - observed[1, c])

        unpack(own, members, write)
        for h in range(HOPS):
            c = table[at.listed + h]
            values[1, c] = values[1, c] + terms[HOPS - 1 - h].astype(F32)
        half[...] = values[1].astype(HALF)
        for h in range(HOPS):
            c = table[at.reader + h]
            sent[h][...] = dot_n(half[c], jac[1, c, table[at.block + h]]).astype(HALF)


def scatter(source, table, jac, step, acc, blocks, c):
    spread = dot_n(source, row_of(jac, step, c, blocks))
    lev = acc.shape[2]
    for k in range(blocks):
        target = table[c * blocks + k]
        acc[target] = acc[target] + spread[:, k * lev : (k + 1) * lev]


def retreat_kernel(
    turn, at, half, table, damp, states, observed, weight, jac, _, values, acc, half1, acc1
):
    columns = half.shape[0]

    @pl.when(table[at.turn] == turn)
    def _():
        acc1[columns:] = jnp.zeros((HOPS,) + acc1.shape[1:], F32)

        def start(c):
            miss = weight[pl.ds(c, 1), :] * (states[0, c] - observed[0, c])
            acc1[c] = damp[pl.ds(c, 1), :] * values[1, c] + miss

        over_columns(columns, start)
        over_columns(
            columns, lambda c: scatter(half[c], table, jac, 1, acc1, at.blocks, c)
        )
        values[0] = acc1[:columns]
        half1[...] = acc1[:columns].astype(HALF)
        for h in range(HOPS):
            half1[table[at.listed + h]] = jnp.zeros(half1.shape[1:], HALF)
        acc[...] = jnp.zeros(acc.shape, F32)
        over_columns(
            columns, lambda c: scatter(half1[c], table, jac, 0, acc, at.blocks, c)
        )


def leave_back_kernel(
    turn, at, u3, u2, u1, u0, table, damp, partial, jac, _, values, own, t0, t1, t2, t3, acc
):
    columns, members = values.shape[1:3]

    @pl.when(table[at.turn] == turn)
    def _():
        for h, term in enumerate((u0, u1, u2, u3)):
            c = table[at.listed + h]
            values[0, c] = values[0, c] + term[...].astype(F32)
        acc[...] = partial[...]
        for h in range(HOPS):
            c = table[at.listed + h]
            source = jnp.where(table[at.first + h] == 1, values[0, c], 0.0).astype(HALF)
            scatter(source, table, jac, 0, acc, at.blocks, c)
        pack(own, members, lambda c: acc[c] + damp[pl.ds(c, 1), :] * values[0, c])
        for h, out in enumerate((t0, t1, t2, t3)):
            out[...] = acc[columns + h].astype(HALF)


def on_device(
    forcing, observed, jacobian, block_index, send_list, damping, error_weight, forcing_weight
):
    turns = lax.axis_size("tm")
    parts = lax.axis_size("space")
    columns, members, lev = forcing.shape[1:]
    blocks = jacobian.shape[2]
    at = Table(columns, blocks)

    def within(piece, by):
        return lax.ppermute(piece, "space", [(i, (i + by) % parts) for i in range(parts)])

    def exchanged(pieces, sign):
        arrived = [None] * HOPS
        for h in reversed(range(HOPS)):
            arrived[h] = within(pieces[h], sign * OFFSETS[h])
        return arrived

    def handed(piece, turn, ahead):
        route = [(s * turns + turn, s * turns + turn + ahead) for s in range(parts)]
        return lax.ppermute(piece, ("space", "tm"), route)

    flat = block_index.reshape(-1)
    wanted = columns + jnp.arange(HOPS, dtype=jnp.int32)
    place = jnp.argmax(flat[None, :] == wanted[:, None], axis=1).astype(jnp.int32)
    listed = send_list.reshape(-1)
    same = listed[:, None] == listed[None, :]
    earlier = jnp.arange(HOPS)[None, :] < jnp.arange(HOPS)[:, None]
    first = 1 - jnp.any(same & earlier, axis=1).astype(jnp.int32)
    plane = lax.axis_index("tm").astype(jnp.int32)[None]
    table = jnp.concatenate([flat, listed, place // blocks, place % blocks, first, plane])

    border = jax.ShapeDtypeStruct((members, lev), HALF)
    borders = [border] * HOPS
    packed = jax.ShapeDtypeStruct((columns * members, lev), F32)
    pair = jax.ShapeDtypeStruct(forcing.shape, F32)
    whole = jax.ShapeDtypeStruct((columns, members, lev), F32)
    more = columns + HOPS

    def call(kernel, turn, operands, smem, outs, alias, scratch, dots):
        specs = [VMEM] * len(operands)
        specs[smem] = SMEM
        return pl.pallas_call(
            functools.partial(kernel, turn, at),
            out_shape=outs,
            in_specs=specs,
            out_specs=[VMEM] * len(outs),
            scratch_shapes=scratch,
            input_output_aliases=alias,
            compiler_params=pltpu.CompilerParams(vmem_limit_bytes=20 * 2**20),
            cost_estimate=pl.CostEstimate(
                flops=2 * dots * members * lev * lev * 16,
                bytes_accessed=dots * lev * lev * 2,
                transcendentals=0,
            ),
        )(*operands)

    own = jnp.zeros(packed.shape, F32)
    received = jnp.zeros((HOPS, members, lev), HALF)
    states = jnp.zeros(pair.shape, F32)
    for turn in range(turns):
        state, half, *sent = call(
            enter_kernel,
            turn,
            [own, received, table, damping, forcing, jacobian],
            2,
            [whole, jax.ShapeDtypeStruct((more, members, lev), HALF)] + borders,
            {},
            [],
            HOPS * blocks,
        )
        arrived = exchanged(sent, 1)
        (states,) = call(
            advance_kernel,
            turn,
            [state, half, table, damping, forcing, jacobian, states],
            2,
            [pair],
            {6: 0},
            [pltpu.VMEM((more, members, lev), HALF)],
            2 * columns * blocks,
        )
        states, own, *sent = call(
            leave_kernel,
            turn,
            [*arrived[::-1], table, jacobian, states],
            4,
            [pair, packed] + borders,
            {6: 0},
            [],
            HOPS,
        )
        if turn < turns - 1:
            own = handed(own, turn, 1)
            sides = exchanged(sent, 1)
            received = handed(jnp.stack(sides[::-1]), turn, 1)

    own = jnp.zeros(packed.shape, F32)
    received = jnp.zeros((HOPS, members, lev), HALF)
    values = jnp.zeros(pair.shape, F32)
    for turn in reversed(range(turns)):
        values, half, *sent = call(
            enter_back_kernel,
            turn,
            [own, received, table, states, observed, error_weight, jacobian, values],
            2,
            [pair, jax.ShapeDtypeStruct((columns, members, lev), HALF)] + borders,
            {7: 0},
            [],
            HOPS,
        )
        arrived = exchanged(sent, -1)
        values, partial = call(
            retreat_kernel,
            turn,
            [half, table, damping, states, observed, error_weight, jacobian, values],
            1,
            [pair, jax.ShapeDtypeStruct((more, members, lev), F32)],
            {7: 0},
            [
                pltpu.VMEM((columns, members, lev), HALF),
                pltpu.VMEM((more, members, lev), F32),
            ],
            2 * columns * blocks,
        )
        values, own, *sent = call(
            leave_back_kernel,
            turn,
            [*arrived[::-1], table, damping, partial, jacobian, values],
            4,
            [pair, packed] + borders,
            {8: 0},
            [pltpu.VMEM((more, members, lev), F32)],
            HOPS * blocks,
        )
        if turn > 0:
            own = handed(own, turn, -1)
            sides = exchanged(sent, -1)
            received = handed(jnp.stack(sides[::-1]), turn, -1)

    gradient = forcing_weight * forcing + values
    return states, gradient


def solution(mesh):
    in_specs = (
        P("tm", "space", None, None),
        P("tm", "space", None, None),
        P("tm", "space", None, None, None),
        P("space", None),
        P("space", None),
        P("space", None),
        P("space", None),
        P(),
    )
    out_specs = (P("tm", "space", None, None), P("tm", "space", None, None))
    return jax.shard_map(
        on_device, mesh=mesh, in_specs=in_specs, out_specs=out_specs, check_vma=False
    )
```

```python
import functools

import jax
import jax.numpy as jnp
from jax import lax
from jax.experimental import pallas as pl
from jax.experimental.pallas import tpu as pltpu
from jax.sharding import PartitionSpec as P

OFFSETS = (1, -1, 2, -2)
HOPS = len(OFFSETS)
UNROLL = 6
HALF = jnp.bfloat16
F32 = jnp.float32

VMEM = pl.BlockSpec(memory_space=pltpu.VMEM)
SMEM = pl.BlockSpec(memory_space=pltpu.SMEM)


class Table:
    def __init__(self, columns, blocks):
        self.blocks = blocks
        self.listed = columns * blocks
        self.reader = self.listed + HOPS
        self.block = self.reader + HOPS
        self.first = self.block + HOPS
        self.turn = self.first + HOPS


def dot_t(x, w):
    return lax.dot_general(x, w, (((1,), (1,)), ((), ())), preferred_element_type=F32)


def dot_n(x, w):
    return lax.dot_general(x, w, (((1,), (0,)), ((), ())), preferred_element_type=F32)


def row_of(jac, step, c, blocks):
    return jnp.concatenate([jac[step, c, k] for k in range(blocks)], axis=1)


def gathered(source, table, c, blocks):
    return jnp.concatenate([source[table[c * blocks + k]] for k in range(blocks)], axis=1)


def unpack(packed, members, write):
    def body(i, carry):
        both = packed[pl.ds(pl.multiple_of(i * 2 * members, 8), 2 * members), :]
        write(2 * i, both[:members])
        write(2 * i + 1, both[members:])
        return carry

    lax.fori_loop(0, packed.shape[0] // members // 2, body, 0)


def pack(packed, members, read):
    def body(i, carry):
        both = jnp.concatenate([read(2 * i), read(2 * i + 1)], axis=0)
        packed[pl.ds(pl.multiple_of(i * 2 * members, 8), 2 * members), :] = both
        return carry

    lax.fori_loop(0, packed.shape[0] // members // 2, body, 0)


def over_columns(columns, visit):
    def body(i, carry):
        for j in range(UNROLL):
            visit(i * UNROLL + j)
        return carry

    lax.fori_loop(0, columns // UNROLL, body, 0)


def enter_kernel(turn, at, own, r0, r1, r2, r3, table, damp, push, jac, state, half, *sent):
    columns, members, _ = state.shape

    @pl.when(table[at.turn] == turn)
    def _():
        def write(c, value):
            state[c] = value
            half[c] = value.astype(HALF)

        unpack(own, members, write)
        for h, border in enumerate((r0, r1, r2, r3)):
            half[columns + h] = border[...]
        for h in range(HOPS):
            c = table[at.listed + h]
            mixed = dot_t(gathered(half, table, c, at.blocks), row_of(jac, 0, c, at.blocks))
            sent[h][...] = (damp[pl.ds(c, 1), :] * state[c] + mixed + push[0, c]).astype(HALF)


def advance_kernel(turn, at, state, half, table, damp, push, jac, _, states, half2):
    columns = state.shape[0]

    @pl.when(table[at.turn] == turn)
    def _():
        def first(c):
            mixed = dot_t(gathered(half, table, c, at.blocks), row_of(jac, 0, c, at.blocks))
            value = damp[pl.ds(c, 1), :] * state[c] + mixed + push[0, c]
            states[0, c] = value
            half2[c] = value.astype(HALF)

        over_columns(columns, first)
        half2[columns:] = jnp.zeros((HOPS,) + half2.shape[1:], HALF)

        def second(c):
            mixed = dot_t(gathered(half2, table, c, at.blocks), row_of(jac, 1, c, at.blocks))
            states[1, c] = damp[pl.ds(c, 1), :] * states[0, c] + mixed + push[1, c]

        over_columns(columns, second)


def leave_kernel(turn, at, r0, r1, r2, r3, table, jac, _, states, own, *sent):
    members = states.shape[2]

    @pl.when(table[at.turn] == turn)
    def _():
        for h, border in enumerate((r0, r1, r2, r3)):
            c = table[at.reader + h]
            states[1, c] = states[1, c] + dot_t(border[...], jac[1, c, table[at.block + h]])
        pack(own, members, lambda c: states[1, c])
        for h in range(HOPS):
            sent[h][...] = states[1, table[at.listed + h]].astype(HALF)


def enter_back_kernel(
    turn, at, own, u0, u1, u2, u3, table, states, observed, weight, jac, _, values, half, *sent
):
    members = states.shape[2]

    @pl.when(table[at.turn] == turn)
    def _():
        def write(c, value):
            values[1, c] = value + weight[pl.ds(c, 1), :] * (states[1, c] - observed[1, c])

        unpack(own, members, write)
        for h, term in enumerate((u0, u1, u2, u3)):
            c = table[at.listed + h]
            values[1, c] = values[1, c] + term[...].astype(F32)
        half[...] = values[1].astype(HALF)
        for h in range(HOPS):
            c = table[at.reader + h]
            sent[h][...] = dot_n(half[c], jac[1, c, table[at.block + h]]).astype(HALF)


def scatter(source, table, jac, step, acc, blocks, c):
    spread = dot_n(source, row_of(jac, step, c, blocks))
    lev = acc.shape[2]
    for k in range(blocks):
        target = table[c * blocks + k]
        acc[target] = acc[target] + spread[:, k * lev : (k + 1) * lev]


def retreat_kernel(
    turn, at, half, table, damp, states, observed, weight, jac, _, values, acc, half1, acc1
):
    columns = half.shape[0]

    @pl.when(table[at.turn] == turn)
    def _():
        acc1[columns:] = jnp.zeros((HOPS,) + acc1.shape[1:], F32)

        def start(c):
            miss = weight[pl.ds(c, 1), :] * (states[0, c] - observed[0, c])
            acc1[c] = damp[pl.ds(c, 1), :] * values[1, c] + miss

        over_columns(columns, start)
        over_columns(
            columns, lambda c: scatter(half[c], table, jac, 1, acc1, at.blocks, c)
        )
        values[0] = acc1[:columns]
        half1[...] = acc1[:columns].astype(HALF)
        for h in range(HOPS):
            half1[table[at.listed + h]] = jnp.zeros(half1.shape[1:], HALF)
        acc[...] = jnp.zeros(acc.shape, F32)
        over_columns(
            columns, lambda c: scatter(half1[c], table, jac, 0, acc, at.blocks, c)
        )


def leave_back_kernel(
    turn, at, u0, u1, u2, u3, table, damp, partial, jac, _, values, own, t0, t1, t2, t3, acc
):
    columns, members = values.shape[1:3]

    @pl.when(table[at.turn] == turn)
    def _():
        for h, term in enumerate((u0, u1, u2, u3)):
            c = table[at.listed + h]
            values[0, c] = values[0, c] + term[...].astype(F32)
        acc[...] = partial[...]
        for h in range(HOPS):
            c = table[at.listed + h]
            source = jnp.where(table[at.first + h] == 1, values[0, c], 0.0).astype(HALF)
            scatter(source, table, jac, 0, acc, at.blocks, c)
        pack(own, members, lambda c: acc[c] + damp[pl.ds(c, 1), :] * values[0, c])
        for h, out in enumerate((t0, t1, t2, t3)):
            out[...] = acc[columns + h].astype(HALF)


def on_device(
    forcing, observed, jacobian, block_index, send_list, damping, error_weight, forcing_weight
):
    turns = lax.axis_size("tm")
    parts = lax.axis_size("space")
    columns, members, lev = forcing.shape[1:]
    blocks = jacobian.shape[2]
    at = Table(columns, blocks)

    def within(piece, by):
        return lax.ppermute(piece, "space", [(i, (i + by) % parts) for i in range(parts)])

    def diagonal(piece, by, ahead):
        route = [
            (s * turns + t, (s + by) % parts * turns + (t + ahead) % turns)
            for s in range(parts)
            for t in range(turns)
        ]
        return lax.ppermute(piece, ("space", "tm"), route)

    flat = block_index.reshape(-1)
    wanted = columns + jnp.arange(HOPS, dtype=jnp.int32)
    place = jnp.argmax(flat[None, :] == wanted[:, None], axis=1).astype(jnp.int32)
    listed = send_list.reshape(-1)
    same = listed[:, None] == listed[None, :]
    earlier = jnp.arange(HOPS)[None, :] < jnp.arange(HOPS)[:, None]
    first = 1 - jnp.any(same & earlier, axis=1).astype(jnp.int32)
    plane = lax.axis_index("tm").astype(jnp.int32)[None]
    table = jnp.concatenate([flat, listed, place // blocks, place % blocks, first, plane])

    border = jax.ShapeDtypeStruct((members, lev), HALF)
    borders = [border] * HOPS
    packed = jax.ShapeDtypeStruct((columns * members, lev), F32)
    pair = jax.ShapeDtypeStruct(forcing.shape, F32)
    whole = jax.ShapeDtypeStruct((columns, members, lev), F32)
    more = columns + HOPS

    def call(kernel, turn, operands, smem, outs, alias, scratch, dots):
        specs = [VMEM] * len(operands)
        specs[smem] = SMEM
        return pl.pallas_call(
            functools.partial(kernel, turn, at),
            out_shape=outs,
            in_specs=specs,
            out_specs=[VMEM] * len(outs),
            scratch_shapes=scratch,
            input_output_aliases=alias,
            compiler_params=pltpu.CompilerParams(vmem_limit_bytes=20 * 2**20),
            cost_estimate=pl.CostEstimate(
                flops=2 * dots * members * lev * lev * 16,
                bytes_accessed=dots * lev * lev * 2,
                transcendentals=0,
            ),
        )(*operands)

    own = jnp.zeros(packed.shape, F32)
    received = [jnp.zeros(border.shape, HALF)] * HOPS
    states = jnp.zeros(pair.shape, F32)
    for turn in range(turns):
        state, half, *sent = call(
            enter_kernel,
            turn,
            [own, *received, table, damping, forcing, jacobian],
            5,
            [whole, jax.ShapeDtypeStruct((more, members, lev), HALF)] + borders,
            {},
            [],
            HOPS * blocks,
        )
        arrived = [within(sent[h], OFFSETS[h]) for h in range(HOPS)]
        (states,) = call(
            advance_kernel,
            turn,
            [state, half, table, damping, forcing, jacobian, states],
            2,
            [pair],
            {6: 0},
            [pltpu.VMEM((more, members, lev), HALF)],
            2 * columns * blocks,
        )
        states, own, *sent = call(
            leave_kernel,
            turn,
            [*arrived, table, jacobian, states],
            4,
            [pair, packed] + borders,
            {6: 0},
            [],
            HOPS,
        )
        if turn < turns - 1:
            received = [diagonal(sent[h], OFFSETS[h], 1) for h in range(HOPS)]
            own = diagonal(own, 0, 1)

    own = jnp.zeros(packed.shape, F32)
    received = [jnp.zeros(border.shape, HALF)] * HOPS
    values = jnp.zeros(pair.shape, F32)
    for turn in reversed(range(turns)):
        values, half, *sent = call(
            enter_back_kernel,
            turn,
            [own, *received, table, states, observed, error_weight, jacobian, values],
            5,
            [pair, jax.ShapeDtypeStruct((columns, members, lev), HALF)] + borders,
            {10: 0},
            [],
            HOPS,
        )
        arrived = [within(sent[h], -OFFSETS[h]) for h in range(HOPS)]
        values, partial = call(
            retreat_kernel,
            turn,
            [half, table, damping, states, observed, error_weight, jacobian, values],
            1,
            [pair, jax.ShapeDtypeStruct((more, members, lev), F32)],
            {7: 0},
            [
                pltpu.VMEM((columns, members, lev), HALF),
                pltpu.VMEM((more, members, lev), F32),
            ],
            2 * columns * blocks,
        )
        values, own, *sent = call(
            leave_back_kernel,
            turn,
            [*arrived, table, damping, partial, jacobian, values],
            4,
            [pair, packed] + borders,
            {8: 0},
            [pltpu.VMEM((more, members, lev), F32)],
            HOPS * blocks,
        )
        if turn > 0:
            received = [diagonal(sent[h], -OFFSETS[h], -1) for h in range(HOPS)]
            own = diagonal(own, 0, -1)

    gradient = forcing_weight * forcing + values
    return states, gradient


def solution(mesh):
    in_specs = (
        P("tm", "space", None, None),
        P("tm", "space", None, None),
        P("tm", "space", None, None, None),
        P("space", None),
        P("space", None),
        P("space", None),
        P("space", None),
        P(),
    )
    out_specs = (P("tm", "space", None, None), P("tm", "space", None, None))
    return jax.shard_map(
        on_device, mesh=mesh, in_specs=in_specs, out_specs=out_specs, check_vma=False
    )
```
